256 devices in a mesh: depth: 16 (over x, y), tile: 16 (over z, core).
Axes of the slice: x: 4, y: 4, z: 8, core: 2. Of those that a mesh axis runs over, the one named last changes fastest.
Arguments:
- volume: float32 [256, 1024, 2048], P('depth', 'tile'), may hold values from -6 to 6
- entry_depth: int32 [1024, 2048], P('tile'), may hold values from 0 to 127
- light_dir: float32 [3], replicated, may hold values from 0.2 to 1
- transfer: float32 [4, 3], replicated, may hold values from -6 to 6
Outputs:
- frame_rgba: float32 [4, 1024, 2048], P(None, 'tile', 'depth')
The draws below stay inside these ranges and needn't reach their ends.
All inputs are finite; a program needn't handle non-finite values.
Results may differ from the reference program's by a relative error of at most 0.0003.
Values sent between devices are 32-bit elements; how exact they have to be, the bound alone decides.
No kernel may reach another device: no remote copies, remote signals or barrier semaphores. Data moves between devices by JAX's collectives and lax.ppermute only.
A program may use at most 128 MiB of HBM per device.

```python
import jax
import jax.numpy as jnp
from jax import lax

TX = 64
NY = 2048
NZ = 256
NX = 1024


def set_ends(values, own_key, least, high):
    index_at = [jax.random.randint(jax.random.fold_in(own_key, axis), (), 0, length) for axis, length in enumerate(values.shape)]
    longest = values.shape.index(max(values.shape))
    beside = index_at[:longest] + [(index_at[longest] + 1) % values.shape[longest]] + index_at[longest + 1:]
    return values.at[tuple(index_at)].set(least).at[tuple(beside)].set(high)


def block_scale(key, dims, cuts, least, high):
    def one(axis_at, blocks):
        draws = jax.random.uniform(jax.random.fold_in(jax.random.fold_in(key, 6), axis_at), (blocks,), jnp.float32, least / len(cuts), high / len(cuts))
        return jnp.repeat(jnp.exp(draws), dims[axis_at] // blocks).reshape((-1,) + (1,) * (len(dims) - axis_at - 1))

    level = one(*cuts[0])
    for cut in cuts[1:]:
        level = level * one(*cut)
    return level


def noise(rng, shape, width, limit, shards=(), kind=jnp.bfloat16):
    gain = block_scale(rng, shape, shards, -0.22, 0.18) if shards else 1.0
    values = jax.random.normal(rng, shape, jnp.float32) * width * gain
    return jnp.minimum(jnp.maximum(values, -limit), limit).astype(kind)


def setup_inputs(seed: int = 0) -> dict:
    streams_of = jax.random.split(jax.random.key(seed), 5)
    volume = noise(streams_of[0], (NZ, NX, NY), 1.0, 6.0, ((0, 16), (1, 16)), jnp.float32)
    entry_depth = set_ends(jax.random.randint(streams_of[1], (NX, NY), 0, NZ // 2), jax.random.fold_in(streams_of[1], 1), 0, (NZ // 2) - 1).astype(jnp.int32)
    light_dir = jnp.clip(jax.random.uniform(streams_of[2], (3,), jnp.float32, 0.2, 1.0), 0.2, 1.0)
    transfer = noise(streams_of[3], (4, 3), 1.5, 6.0, (), jnp.float32)
    return dict(volume=volume, entry_depth=entry_depth, light_dir=light_dir, transfer=transfer)


def emission(padded, depth_pos, entry_depth, light_dir, transfer, depth_total):
    centre = padded[1:-1, 1:-1, 1:-1]
    grad_z = (padded[2:, 1:-1, 1:-1] - padded[:-2, 1:-1, 1:-1]) * 0.5
    grad_x = (padded[1:-1, 2:, 1:-1] - padded[1:-1, :-2, 1:-1]) * 0.5
    grad_y = (padded[1:-1, 1:-1, 2:] - padded[1:-1, 1:-1, :-2]) * 0.5
    grad_norm = jnp.sqrt(grad_z * grad_z + grad_x * grad_x + grad_y * grad_y + 1.0)
    light_norm = jnp.sqrt(jnp.sum(light_dir * light_dir))
    facing = jnp.abs(light_dir[0] * grad_z + light_dir[1] * grad_x + light_dir[2] * grad_y)
    shading = 0.3 + 0.7 * facing / (grad_norm * light_norm)
    opacity = 4.0 / depth_total * jax.nn.sigmoid(transfer[3, 0] * centre + transfer[3, 1] * grad_norm + transfer[3, 2])
    opacity = jnp.where(depth_pos[:, None, None] >= entry_depth[None], opacity, 0.0)
    colors = jnp.stack([shading * jax.nn.sigmoid(transfer[k, 0] * centre + transfer[k, 1] * grad_norm + transfer[k, 2]) for k in range(3)])
    return (opacity, colors)

def composite(opacity, colors):
    logs = jnp.log1p(-opacity)
    transmit = jnp.exp(jnp.cumsum(logs, axis=0) - logs)
    weight = transmit * opacity
    shaded = lax.optimization_barrier(jnp.sum(weight[None] * colors, axis=1))
    return jnp.concatenate([shaded, lax.optimization_barrier(jnp.sum(weight, axis=0))[None]], axis=0)

def reference(volume, entry_depth, light_dir, transfer):
    padded = jnp.pad(volume, 1)
    depth_pos = jnp.arange(NZ, dtype=jnp.int32)

    def one_block(block):
        row_start = (block * TX).astype(jnp.int32)
        zero = jnp.zeros((), jnp.int32)
        piece = lax.dynamic_slice(padded, (zero, row_start, zero), (NZ + 2, TX + 2, NY + 2))
        entries = lax.dynamic_slice(entry_depth, (row_start, zero), (TX, NY))
        opacity, colors = emission(piece, depth_pos, entries, light_dir, transfer, float(NZ))
        return composite(opacity, colors)
    blocks = lax.map(one_block, jnp.arange(NX // TX, dtype=jnp.int32))
    return jnp.transpose(blocks, (1, 0, 2, 3)).reshape(4, NX, NY)
```

```python
import functools

import jax
import jax.numpy as jnp
from jax import lax
from jax.experimental import pallas as pl
from jax.experimental.pallas import tpu as pltpu
from jax.sharding import PartitionSpec as P

ROW = 8
LANE = 128
LOG2E = 1.4426950408889634


def cast_kernel(depth_total, light, transfer, base, volume, front, back, above, below, entry, out, cells, sems):
    step = pl.program_id(0)
    slabs, rows, columns = volume.shape
    tiles = rows // ROW

    def fetch(tile):
        at = pl.ds(pl.multiple_of(tile * ROW, ROW), ROW)
        to = pl.ds(pl.multiple_of(tile * ROW + ROW, ROW), ROW)
        cols = pl.ds(LANE, columns)
        return (
            pltpu.make_async_copy(volume.at[:, at, :], cells.at[pl.ds(1, slabs), to, cols], sems.at[0, tile]),
            pltpu.make_async_copy(front.at[at, :], cells.at[0, to, cols], sems.at[1, tile]),
            pltpu.make_async_copy(back.at[at, :], cells.at[slabs + 1, to, cols], sems.at[2, tile]),
        )

    def fringe():
        cols = pl.ds(LANE, columns)
        inner = pl.ds(1, slabs)
        return (
            pltpu.make_async_copy(above, cells.at[inner, pl.ds(ROW - 1, 1), cols], sems.at[0, tiles]),
            pltpu.make_async_copy(below, cells.at[inner, pl.ds(ROW + rows, 1), cols], sems.at[1, tiles]),
        )

    @pl.when(step == 0)
    def _():
        for copy in fringe():
            copy.start()
        for tile in range(tiles):
            for copy in fetch(tile):
                copy.start()
        blank = jnp.zeros((rows, LANE), jnp.float32)
        for slab in range(1, slabs + 1):
            cells[slab, ROW : ROW + rows, 0:LANE] = blank
            cells[slab, ROW : ROW + rows, LANE + columns : 2 * LANE + columns] = blank
        for copy in fringe():
            copy.wait()
        for copy in fetch(0):
            copy.wait()

    @pl.when(step < tiles - 1)
    def _():
        for copy in fetch(step + 1):
            copy.wait()

    shape = (ROW, LANE)
    lanes = lax.broadcasted_iota(jnp.int32, shape, 1)
    subs = lax.broadcasted_iota(jnp.int32, shape, 0)
    first_lane, last_lane = lanes == 0, lanes == LANE - 1
    first_sub, last_sub = subs == 0, subs == ROW - 1

    def splat(value):
        return jnp.full(shape, value, jnp.float32)

    l0, l1, l2 = (splat(light[i]) for i in range(3))
    scale = 0.35 * lax.rsqrt(l0 * l0 + l1 * l1 + l2 * l2)
    l0, l1, l2 = l0 * scale, l1 * scale, l2 * scale
    hue = [
        (splat(transfer[k, 0] * 0.5), splat(transfer[k, 1] * 0.25), splat(transfer[k, 2] * 0.5))
        for k in range(3)
    ]
    width = jnp.log2(jnp.float32(depth_total / 4.0))
    veil = (
        splat(transfer[3, 0] * -LOG2E),
        splat(transfer[3, 1] * (-0.5 * LOG2E)),
        splat(transfer[3, 2] * -LOG2E + width),
    )
    row_at = pl.ds(pl.multiple_of(step * ROW + ROW, ROW), ROW)
    row_up = pl.ds(pl.multiple_of(step * ROW, ROW), ROW)
    row_dn = pl.ds(pl.multiple_of(step * ROW + 2 * ROW, ROW), ROW)
    origin = base[0]

    def column(k, carry):
        col = pl.ds(pl.multiple_of(k * LANE + LANE, LANE), LANE)
        col_lf = pl.ds(pl.multiple_of(k * LANE, LANE), LANE)
        col_rt = pl.ds(pl.multiple_of(k * LANE + 2 * LANE, LANE), LANE)
        start = entry[:, pl.ds(pl.multiple_of(k * LANE, LANE), LANE)] - origin
        alpha = jnp.zeros(shape, jnp.float32)
        plain = jnp.zeros(shape, jnp.float32)
        tinted = [jnp.zeros(shape, jnp.float32) for _ in range(3)]
        before = cells[0, row_at, col]
        here = cells[1, row_at, col]
        for slab in range(slabs):
            after = cells[slab + 2, row_at, col]
            up = pltpu.roll(jnp.where(last_sub, cells[slab + 1, row_up, col], here), 1, 0)
            dn = pltpu.roll(jnp.where(first_sub, cells[slab + 1, row_dn, col], here), ROW - 1, 0)
            lf = pltpu.roll(jnp.where(last_lane, cells[slab + 1, row_at, col_lf], here), 1, 1)
            rt = pltpu.roll(jnp.where(first_lane, cells[slab + 1, row_at, col_rt], here), LANE - 1, 1)
            gz, gx, gy = after - before, dn - up, rt - lf
            square = gz * gz + gx * gx + gy * gy + 4.0
            inverse = lax.rsqrt(square)
            norm = square * inverse
            shade = 0.15 + jnp.abs(l0 * gz + l1 * gx + l2 * gy) * inverse
            dim = jnp.exp2(veil[0] * here + veil[1] * norm + veil[2])
            root = lax.rsqrt(dim + depth_total / 4.0)
            opacity = jnp.where(start <= slab, root * root, 0.0)
            weight = (1.0 - alpha) * opacity
            alpha = alpha + weight
            lit = weight * shade
            plain = plain + lit
            for c in range(3):
                a, b, o = hue[c]
                tinted[c] = tinted[c] + lit * jnp.tanh(a * here + b * norm + o)
            before, here = here, after
        for c in range(3):
            out[k, c] = plain + tinted[c]
        out[k, 3] = alpha
        return carry

    lax.fori_loop(0, columns // LANE, column, 0)


def cast(volume, front, back, above, below, entry, light, transfer, base, depth_total):
    slabs, rows, columns = volume.shape
    pieces = columns // LANE
    smem = pl.BlockSpec(memory_space=pltpu.SMEM)
    hbm = pl.BlockSpec(memory_space=pl.ANY)
    return pl.pallas_call(
        functools.partial(cast_kernel, depth_total),
        grid=(rows // ROW,),
        in_specs=[smem, smem, smem, hbm, hbm, hbm, hbm, hbm, pl.BlockSpec((ROW, columns), lambda i: (i, 0))],
        out_specs=pl.BlockSpec((pieces, 4, ROW, LANE), lambda i: (0, 0, i, 0)),
        out_shape=jax.ShapeDtypeStruct((pieces, 4, rows, LANE), jnp.float32),
        scratch_shapes=[
            pltpu.VMEM((slabs + 2, rows + 2 * ROW, columns + 2 * LANE), jnp.float32),
            pltpu.SemaphoreType.DMA((3, rows // ROW + 1)),
        ],
        compiler_params=pltpu.CompilerParams(dimension_semantics=("arbitrary",), vmem_limit_bytes=40 * 2**20),
        cost_estimate=pl.CostEstimate(flops=slabs * rows * columns * 60, bytes_accessed=slabs * rows * columns * 5, transcendentals=slabs * rows * columns * 6),
        name="cast",
    )(light, transfer, base, volume, front, back, above, below, entry)


def merge_kernel(parts, out):
    count = parts.shape[0]
    clear = 1.0 - parts[0, 3]
    total = [parts[0, c] for c in range(4)]
    for d in range(1, count):
        total = [total[c] + clear * parts[d, c] for c in range(4)]
        clear = clear * (1.0 - parts[d, 3])
    for c in range(4):
        out[c] = total[c]


def merge(parts):
    count, channels, rows, cols = parts.shape
    return pl.pallas_call(
        merge_kernel,
        grid=(rows // ROW,),
        in_specs=[pl.BlockSpec((count, channels, ROW, cols), lambda i: (0, 0, i, 0))],
        out_specs=pl.BlockSpec((channels, ROW, cols), lambda i: (0, i, 0)),
        out_shape=jax.ShapeDtypeStruct((channels, rows, cols), jnp.float32),
        name="merge",
    )(parts)


def local(volume, entry_depth, light_dir, transfer):
    slabs, rows, columns = volume.shape
    groups = lax.axis_size("depth")
    up = [(i, i + 1) for i in range(lax.axis_size("depth") - 1)]
    up_t = [(i, i + 1) for i in range(lax.axis_size("tile") - 1)]
    front = lax.ppermute(volume[slabs - 1], "depth", up)
    back = lax.ppermute(volume[0], "depth", [(b, a) for a, b in up])
    above = lax.ppermute(volume[:, rows - 1 :], "tile", up_t)
    below = lax.ppermute(volume[:, :1], "tile", [(b, a) for a, b in up_t])
    base = jnp.full((1,), lax.axis_index("depth") * slabs, jnp.int32)
    parts = cast(volume, front, back, above, below, entry_depth, light_dir, transfer, base, float(slabs * groups))
    parts = lax.all_to_all(parts, "depth", 0, 0)
    return merge(parts)


def solution(mesh):
    placed = (P("depth", "tile", None), P("tile", None), P(), P())
    return jax.shard_map(
        local, mesh=mesh, in_specs=placed, out_specs=P(None, "tile", "depth"), check_vma=False
    )
```

```python
import functools

import jax
import jax.numpy as jnp
from jax import lax
from jax.experimental import pallas as pl
from jax.experimental.pallas import tpu as pltpu
from jax.sharding import PartitionSpec as P

ROW = 8
LANE = 128
LOG2E = 1.4426950408889634
CHANNELS = 4
VMEM = pl.BlockSpec(memory_space=pltpu.VMEM)
SMEM = pl.BlockSpec(memory_space=pltpu.SMEM)
HBM = pl.BlockSpec(memory_space=pl.ANY)


def edges_kernel(volume, last_slab, first_slab, last_row, first_row, sems):
    slabs, rows, _ = volume.shape
    copies = [
        pltpu.make_async_copy(volume.at[slabs - 1], last_slab, sems.at[0]),
        pltpu.make_async_copy(volume.at[0], first_slab, sems.at[1]),
        pltpu.make_async_copy(volume.at[:, pl.ds(rows - 1, 1), :], last_row, sems.at[2]),
        pltpu.make_async_copy(volume.at[:, pl.ds(0, 1), :], first_row, sems.at[3]),
    ]
    for copy in copies:
        copy.start()
    for copy in copies:
        copy.wait()


def edges(volume):
    slabs, rows, columns = volume.shape
    slab = jax.ShapeDtypeStruct((rows, columns), jnp.float32)
    row = jax.ShapeDtypeStruct((slabs, 1, columns), jnp.float32)
    return pl.pallas_call(
        edges_kernel,
        in_specs=[HBM],
        out_specs=[VMEM] * 4,
        out_shape=[slab, slab, row, row],
        scratch_shapes=[pltpu.SemaphoreType.DMA((4,))],
        compiler_params=pltpu.CompilerParams(vmem_limit_bytes=50 * 2**20),
        cost_estimate=pl.CostEstimate(flops=0, bytes_accessed=4 * 2**20, transcendentals=0),
        name="edges",
    )(volume)


def constants(light, transfer, depth_total):
    def splat(value):
        return jnp.full((ROW, LANE), value, jnp.float32)

    toward = [splat(light[i]) for i in range(3)]
    scale = 0.35 * lax.rsqrt(toward[0] * toward[0] + toward[1] * toward[1] + toward[2] * toward[2])
    toward = [value * scale for value in toward]
    hues = [
        (splat(transfer[k, 0] * 0.5), splat(transfer[k, 1] * 0.25), splat(transfer[k, 2] * 0.5))
        for k in range(3)
    ]
    veil = (
        splat(transfer[3, 0] * -LOG2E),
        splat(transfer[3, 1] * (-0.5 * LOG2E)),
        splat(transfer[3, 2] * -LOG2E) + jnp.log2(splat(depth_total / 4.0)),
    )
    return toward, hues, veil


class Shader:
    def __init__(self, light, transfer, depth_total):
        self.toward, self.hues, self.veil = constants(light, transfer, depth_total)
        self.bound = depth_total / 4.0

    def lateral(self, gx, gy):
        return gx * gx + gy * gy + 4.0, self.toward[1] * gx + self.toward[2] * gy

    def add(self, state, visible, here, gz, square, facing):
        alpha, plain, tinted = state
        square = square + gz * gz
        inverse = lax.rsqrt(square)
        norm = square * inverse
        shade = 0.15 + jnp.abs(self.toward[0] * gz + facing) * inverse
        dim = jnp.exp2(self.veil[0] * here + self.veil[1] * norm + self.veil[2])
        root = lax.rsqrt(dim + self.bound)
        opacity = jnp.where(visible, root * root, 0.0)
        weight = opacity - alpha * opacity
        lit = weight * shade
        tinted = [
            tinted[k] + lit * jnp.tanh(self.hues[k][0] * here + self.hues[k][1] * norm + self.hues[k][2])
            for k in range(3)
        ]
        return alpha + weight, plain + lit, tinted


class Bricks:
    def __init__(self, cells, lanes):
        self.cells = cells
        self.left_edge, self.right_edge = lanes == 0, lanes == LANE - 1

    def load(self, piece, slab, at, shift=0, aside=0):
        return self.cells[piece + 1 + aside, slab, pl.ds(at + shift, ROW), :]

    def lateral(self, shader, piece, slab, at, here):
        lf = pltpu.roll(jnp.where(self.right_edge, self.load(piece, slab, at, 0, -1), here), 1, 1)
        rt = pltpu.roll(jnp.where(self.left_edge, self.load(piece, slab, at, 0, 1), here), LANE - 1, 1)
        return shader.lateral(self.load(piece, slab, at, 1) - self.load(piece, slab, at, -1), rt - lf)

    def clear_sides(self, at, rows):
        pieces, slabs = self.cells.shape[0] - 2, self.cells.shape[1]
        blank = jnp.zeros((rows, LANE), jnp.float32)
        for slab in range(slabs):
            self.cells[0, slab, at : at + rows] = blank
            self.cells[pieces + 1, slab, at : at + rows] = blank


def middle_kernel(depth_total, light, transfer, base, volume, entry, seen, ends, cells, sems):
    slabs, rows, columns = volume.shape
    pieces = columns // LANE

    def fetch(piece):
        return pltpu.make_async_copy(
            volume.at[:, :, pl.ds(pl.multiple_of(piece * LANE, LANE), LANE)],
            cells.at[piece + 1],
            sems.at[piece],
        )

    def begin(piece, carry):
        fetch(piece).start()
        return carry

    lax.fori_loop(0, pieces, begin, 0)
    bricks = Bricks(cells, lax.broadcasted_iota(jnp.int32, (ROW, LANE), 1))
    bricks.clear_sides(ROW, rows - 2 * ROW)
    shader = Shader(light, transfer, depth_total)
    origin = base[0]
    zero = jnp.zeros((ROW, LANE), jnp.float32)
    fetch(0).wait()

    def column(piece, carry):
        @pl.when(piece < pieces - 1)
        def _():
            fetch(piece + 1).wait()

        cols = pl.ds(pl.multiple_of(piece * LANE, LANE), LANE)
        for at in range(ROW, rows - ROW, ROW):
            start = entry[at : at + ROW, cols] - origin
            state = (zero, zero, [zero] * 3)
            before, here = bricks.load(piece, 0, at), bricks.load(piece, 1, at)
            for slab in range(1, slabs - 1):
                after = bricks.load(piece, slab + 1, at)
                side = bricks.lateral(shader, piece, slab, at, here)
                state = shader.add(state, start <= slab, here, after - before, *side)
                before, here = here, after
            to = pl.ds(at - ROW, ROW)
            for k in range(3):
                seen[piece, k, to, :] = state[1] + state[2][k]
            seen[piece, 3, to, :] = state[0]
            for end, (slab, inner) in enumerate(((0, 1), (slabs - 1, slabs - 2))):
                side = bricks.lateral(shader, piece, slab, at, bricks.load(piece, slab, at))
                for k, value in enumerate((*side, bricks.load(piece, inner, at))):
                    ends[end, k, piece, to, :] = value
        return carry

    lax.fori_loop(0, pieces, column, 0)


def finish_kernel(
    depth_total, light, transfer, base, volume, entry, above, below, front, back, near, far, seen, ends, out, upper, lower, sems
):
    slabs, rows, columns = volume.shape
    pieces = columns // LANE
    at_last = rows - ROW

    def fetches(piece):
        cols = pl.ds(pl.multiple_of(piece * LANE, LANE), LANE)
        return (
            pltpu.make_async_copy(
                volume.at[:, pl.ds(0, 2 * ROW), cols], upper.at[piece + 1, :, pl.ds(ROW, 2 * ROW), :], sems.at[0, piece]
            ),
            pltpu.make_async_copy(
                volume.at[:, pl.ds(rows - 2 * ROW, 2 * ROW), cols], lower.at[piece + 1, :, pl.ds(0, 2 * ROW), :], sems.at[1, piece]
            ),
        )

    def begin(piece, carry):
        for copy in fetches(piece):
            copy.start()
        return carry

    lax.fori_loop(0, pieces, begin, 0)
    shader = Shader(light, transfer, depth_total)
    lanes = lax.broadcasted_iota(jnp.int32, (ROW, LANE), 1)
    tops, bottoms = Bricks(upper, lanes), Bricks(lower, lanes)
    for bricks in (tops, bottoms):
        bricks.clear_sides(ROW, ROW)
    origin = base[0]
    zero = jnp.zeros((ROW, LANE), jnp.float32)

    def closing(piece, carry):
        cols = pl.ds(pl.multiple_of(piece * LANE, LANE), LANE)
        for row in range(ROW, at_last, ROW):
            at, src = pl.ds(row, ROW), pl.ds(row - ROW, ROW)
            start = entry[at, cols] - origin
            square, facing, inner = (ends[0, k, piece, src, :] for k in range(3))
            alpha, plain, tinted = shader.add(
                (zero, zero, [zero] * 3), start <= 0, near[at, cols], inner - front[at, cols], square, facing
            )
            clear = 1.0 - alpha
            tinted = [tinted[k] + plain + clear * seen[piece, k, src, :] for k in range(3)]
            alpha = alpha + clear * seen[piece, 3, src, :]
            square, facing, inner = (ends[1, k, piece, src, :] for k in range(3))
            alpha, plain, tinted = shader.add(
                (alpha, zero, tinted), start <= slabs - 1, far[at, cols], back[at, cols] - inner, square, facing
            )
            for k in range(3):
                out[piece, k, at, :] = plain + tinted[k]
            out[piece, 3, at, :] = alpha
        return carry

    lax.fori_loop(0, pieces, closing, 0)

    def ready(piece, carry):
        for copy in fetches(piece):
            copy.wait()
        cols = pl.ds(pl.multiple_of(piece * LANE, LANE), LANE)
        for slab in range(slabs):
            upper[piece + 1, slab, ROW - 1 : ROW, :] = above[slab, :, cols]
            lower[piece + 1, slab, 2 * ROW : 2 * ROW + 1, :] = below[slab, :, cols]
        return carry

    lax.fori_loop(0, pieces, ready, 0)

    def rims(piece, carry):
        cols = pl.ds(pl.multiple_of(piece * LANE, LANE), LANE)
        for bricks, row in ((tops, 0), (bottoms, at_last)):
            at = pl.ds(row, ROW)
            start = entry[at, cols] - origin
            alpha, plain, tinted = zero, zero, [zero] * 3
            before, here = front[at, cols], bricks.load(piece, 0, ROW)
            for slab in range(slabs):
                after = back[at, cols] if slab == slabs - 1 else bricks.load(piece, slab + 1, ROW)
                side = bricks.lateral(shader, piece, slab, ROW, here)
                alpha, plain, tinted = shader.add((alpha, plain, tinted), start <= slab, here, after - before, *side)
                before, here = here, after
            for k in range(3):
                out[piece, k, at, :] = plain + tinted[k]
            out[piece, 3, at, :] = alpha
        return carry

    lax.fori_loop(0, pieces, rims, 0, unroll=2)


def middle(volume, entry, light, transfer, base, depth_total):
    slabs, rows, columns = volume.shape
    pieces, inner = columns // LANE, rows - 2 * ROW
    work = (slabs - 2) * inner * columns
    return pl.pallas_call(
        functools.partial(middle_kernel, depth_total),
        in_specs=[SMEM, SMEM, SMEM, HBM, VMEM],
        out_specs=[VMEM, VMEM],
        out_shape=[
            jax.ShapeDtypeStruct((pieces, CHANNELS, inner, LANE), jnp.float32),
            jax.ShapeDtypeStruct((2, 3, pieces, inner, LANE), jnp.float32),
        ],
        scratch_shapes=[
            pltpu.VMEM((pieces + 2, slabs, rows, LANE), jnp.float32),
            pltpu.SemaphoreType.DMA((pieces,)),
        ],
        compiler_params=pltpu.CompilerParams(vmem_limit_bytes=46 * 2**20),
        cost_estimate=pl.CostEstimate(flops=work * 60, bytes_accessed=work * 4, transcendentals=work * 6),
        name="middle",
    )(light, transfer, base, volume, entry)


def finish(volume, entry, above, below, front, back, near, far, seen, ends, light, transfer, base, depth_total):
    slabs, rows, columns = volume.shape
    pieces = columns // LANE
    work = slabs * 2 * ROW * columns + 2 * rows * columns
    rim = pltpu.VMEM((pieces + 2, slabs, 3 * ROW, LANE), jnp.float32)
    return pl.pallas_call(
        functools.partial(finish_kernel, depth_total),
        in_specs=[SMEM] * 3 + [HBM] + [VMEM] * 9,
        out_specs=VMEM,
        out_shape=jax.ShapeDtypeStruct((pieces, CHANNELS, rows, LANE), jnp.float32),
        scratch_shapes=[rim, rim, pltpu.SemaphoreType.DMA((2, pieces))],
        compiler_params=pltpu.CompilerParams(vmem_limit_bytes=40 * 2**20),
        cost_estimate=pl.CostEstimate(flops=work * 60, bytes_accessed=work * 4, transcendentals=work * 6),
        name="finish",
    )(light, transfer, base, volume, entry, above, below, front, back, near, far, seen, ends)


def merge_kernel(parts, out):
    count, _, rows, _ = parts.shape

    def rows_of(tile, carry):
        at = pl.ds(pl.multiple_of(tile * ROW, ROW), ROW)
        clear = 1.0 - parts[0, 3, at, :]
        total = [parts[0, k, at, :] for k in range(CHANNELS)]
        for d in range(1, count):
            total = [total[k] + clear * parts[d, k, at, :] for k in range(CHANNELS)]
            clear = clear - clear * parts[d, 3, at, :]
        for k in range(CHANNELS):
            out[k, at, :] = total[k]
        return carry

    lax.fori_loop(0, rows // ROW, rows_of, 0, unroll=2)


def merge(parts):
    _, channels, rows, cols = parts.shape
    return pl.pallas_call(
        merge_kernel,
        in_specs=[VMEM],
        out_specs=VMEM,
        out_shape=jax.ShapeDtypeStruct((channels, rows, cols), jnp.float32),
        compiler_params=pltpu.CompilerParams(vmem_limit_bytes=8 * 2**20),
        cost_estimate=pl.CostEstimate(flops=parts.size, bytes_accessed=parts.size * 4, transcendentals=0),
        name="merge",
    )(parts)


def local(volume, entry, light, transfer):
    slabs, _, _ = volume.shape
    groups, tiles = lax.axis_size("depth"), lax.axis_size("tile")
    total = float(slabs * groups)
    up = [(i, i + 1) for i in range(groups - 1)]
    up_t = [(i, i + 1) for i in range(tiles - 1)]
    last_slab, first_slab, last_row, first_row = edges(volume)
    front = lax.ppermute(last_slab, "depth", up)
    back = lax.ppermute(first_slab, "depth", [(b, a) for a, b in up])
    above = lax.ppermute(last_row, "tile", up_t)
    below = lax.ppermute(first_row, "tile", [(b, a) for a, b in up_t])
    base = jnp.full((1,), lax.axis_index("depth") * slabs, jnp.int32)

    seen, ends = middle(volume, entry, light, transfer, base, total)
    parts = finish(
        volume, entry, above, below, front, back, first_slab, last_slab, seen, ends, light, transfer, base, total
    )
    return merge(lax.all_to_all(parts, "depth", 0, 0))


def solution(mesh):
    placed = (P("depth", "tile", None), P("tile", None), P(), P())
    return jax.shard_map(local, mesh=mesh, in_specs=placed, out_specs=P(None, "tile", "depth"), check_vma=False)
```

```python
import functools
import math

import jax
import jax.numpy as jnp
from jax import lax
from jax.experimental import pallas as pl
from jax.experimental.pallas import tpu as pltpu
from jax.sharding import PartitionSpec as P

ROW = 8
LANE = 128
LOG2E = 1.4426950408889634
CHANNELS = 4
VMEM = pl.BlockSpec(memory_space=pltpu.VMEM)
SMEM = pl.BlockSpec(memory_space=pltpu.SMEM)
HBM = pl.BlockSpec(memory_space=pl.ANY)


def edges_kernel(volume, last_slab, first_slab, last_row, first_row, sems):
    slabs, rows, _ = volume.shape
    copies = [
        pltpu.make_async_copy(volume.at[slabs - 1], last_slab, sems.at[0]),
        pltpu.make_async_copy(volume.at[0], first_slab, sems.at[1]),
        pltpu.make_async_copy(volume.at[:, pl.ds(rows - 1, 1), :], last_row, sems.at[2]),
        pltpu.make_async_copy(volume.at[:, pl.ds(0, 1), :], first_row, sems.at[3]),
    ]
    for copy in copies:
        copy.start()
    for copy in copies:
        copy.wait()


def edges(volume):
    slabs, rows, columns = volume.shape
    slab = jax.ShapeDtypeStruct((rows, columns), jnp.float32)
    row = jax.ShapeDtypeStruct((slabs, 1, columns), jnp.float32)
    return pl.pallas_call(
        edges_kernel,
        in_specs=[HBM],
        out_specs=[VMEM] * 4,
        out_shape=[slab, slab, row, row],
        scratch_shapes=[pltpu.SemaphoreType.DMA((4,))],
        compiler_params=pltpu.CompilerParams(vmem_limit_bytes=50 * 2**20),
        cost_estimate=pl.CostEstimate(flops=0, bytes_accessed=4 * 2**20, transcendentals=0),
        name="edges",
    )(volume)


def constants(light, transfer):
    def splat(value):
        return jnp.full((ROW, LANE), value, jnp.float32)

    toward = [splat(light[i]) for i in range(3)]
    scale = 0.35 * lax.rsqrt(toward[0] * toward[0] + toward[1] * toward[1] + toward[2] * toward[2])
    toward = [value * scale for value in toward]
    rows = [[transfer[k, i] * (0.25 if i == 1 else 0.5) for i in range(3)] for k in range(3)]
    rows.append([transfer[3, i] * (-0.5 * LOG2E if i == 1 else -LOG2E) for i in range(3)])
    return toward, rows


def mixing(rows, width):
    size = (CHANNELS * ROW, 10 * ROW)
    line = lax.broadcasted_iota(jnp.int32, size, 0)
    column = lax.broadcasted_iota(jnp.int32, size, 1)
    block, diagonal = column >> 3, (column & 7) == (line & 7)
    shift = jnp.full(size, width, jnp.float32)

    def chosen(i):
        value = jnp.full(size, rows[0][i], jnp.float32)
        for k in range(1, CHANNELS):
            value = jnp.where(line >= k * ROW, rows[k][i], value)
        return value

    def top(value):
        return value.astype(jnp.bfloat16).astype(jnp.float32)

    scale = jnp.where((block & 1) == 0, chosen(0), chosen(1))
    scale = jnp.where(block < 4, top(scale), scale - top(scale))
    offset = chosen(2) + jnp.where(line >= 3 * ROW, shift, 0.0)
    high = top(offset)
    low = top(offset - high)
    offset = jnp.where(column == 8 * ROW, high, jnp.where(column == 8 * ROW + 1, low, offset - high - low))
    mix = jnp.where((block < 8) & diagonal, scale, jnp.where((column >= 8 * ROW) & (column < 8 * ROW + 3), offset, 0.0))
    return mix.astype(jnp.bfloat16)


class Shader:
    def __init__(self, light, transfer, depth_total):
        self.toward, rows = constants(light, transfer)
        self.bound = depth_total / 4.0
        width = math.log2(depth_total / 4.0)
        self.rows = [
            [jnp.full((ROW, LANE), row[i] + (width if (k, i) == (3, 2) else 0.0), jnp.float32) for i in range(3)]
            for k, row in enumerate(rows)
        ]
        self.mix = mixing(rows, width)
        self.ones = jnp.ones((2 * ROW, LANE), jnp.bfloat16)

    def lateral(self, gx, gy):
        return gx * gx + gy * gy + 4.0, self.toward[1] * gx + self.toward[2] * gy

    def look(self, cells):
        pairs, shades = [], []
        for here, gz, square, facing in cells:
            square = square + gz * gz
            inverse = lax.rsqrt(square)
            pairs.append(jnp.concatenate([here, square * inverse], axis=0))
            shades.append(0.15 + jnp.abs(self.toward[0] * gz + facing) * inverse)
        pair = jnp.concatenate(pairs, axis=1)
        high = pair.astype(jnp.bfloat16)
        low = (pair - high.astype(jnp.float32)).astype(jnp.bfloat16)
        ones = jnp.concatenate([self.ones] * len(cells), axis=1)
        terms = jnp.concatenate([high, low, high, low, ones], axis=0)
        args = jnp.dot(self.mix, terms, preferred_element_type=jnp.float32)
        args = [
            [args[k * ROW : (k + 1) * ROW, n * LANE : (n + 1) * LANE] for k in range(CHANNELS)] for n in range(len(cells))
        ]
        return list(zip(shades, args))

    def look_direct(self, here, gz, square, facing):
        square = square + gz * gz
        inverse = lax.rsqrt(square)
        norm = square * inverse
        shade = 0.15 + jnp.abs(self.toward[0] * gz + facing) * inverse
        return shade, [self.rows[k][0] * here + self.rows[k][1] * norm + self.rows[k][2] for k in range(CHANNELS)]

    def add(self, state, visible, shade, args):
        alpha, plain, tinted = state
        root = lax.rsqrt(jnp.exp2(args[3]) + self.bound)
        opacity = jnp.where(visible, root * root, 0.0)
        weight = opacity - alpha * opacity
        lit = weight * shade
        tinted = [tinted[k] + lit * jnp.tanh(args[k]) for k in range(3)]
        return alpha + weight, plain + lit, tinted


class Bricks:
    def __init__(self, cells, lanes):
        self.cells = cells
        self.left_edge, self.right_edge = lanes == 0, lanes == LANE - 1

    def load(self, piece, slab, at, shift=0, aside=0):
        return self.cells[piece + 1 + aside, slab, pl.ds(at + shift, ROW), :]

    def lateral(self, shader, piece, slab, at, here):
        lf = pltpu.roll(jnp.where(self.right_edge, self.load(piece, slab, at, 0, -1), here), 1, 1)
        rt = pltpu.roll(jnp.where(self.left_edge, self.load(piece, slab, at, 0, 1), here), LANE - 1, 1)
        return shader.lateral(self.load(piece, slab, at, 1) - self.load(piece, slab, at, -1), rt - lf)

    def clear_sides(self, at, rows):
        pieces, slabs = self.cells.shape[0] - 2, self.cells.shape[1]
        blank = jnp.zeros((rows, LANE), jnp.float32)
        for slab in range(slabs):
            self.cells[0, slab, at : at + rows] = blank
            self.cells[pieces + 1, slab, at : at + rows] = blank


def middle_kernel(depth_total, light, transfer, base, volume, entry, seen, ends, cells, sems):
    slabs, rows, columns = volume.shape
    pieces = columns // LANE

    def fetch(piece):
        return pltpu.make_async_copy(
            volume.at[:, :, pl.ds(pl.multiple_of(piece * LANE, LANE), LANE)],
            cells.at[piece + 1],
            sems.at[piece],
        )

    def begin(piece, carry):
        fetch(piece).start()
        return carry

    lax.fori_loop(0, pieces, begin, 0)
    bricks = Bricks(cells, lax.broadcasted_iota(jnp.int32, (ROW, LANE), 1))
    bricks.clear_sides(ROW, rows - 2 * ROW)
    shader = Shader(light, transfer, depth_total)
    origin = base[0]
    zero = jnp.zeros((ROW, LANE), jnp.float32)
    fetch(0).wait()

    def column(piece, carry):
        @pl.when(piece < pieces - 1)
        def _():
            fetch(piece + 1).wait()

        cols = pl.ds(pl.multiple_of(piece * LANE, LANE), LANE)
        for at in range(ROW, rows - ROW, ROW):
            start = entry[at : at + ROW, cols] - origin
            state = (zero, zero, [zero] * 3)
            cells_here = []
            before, here = bricks.load(piece, 0, at), bricks.load(piece, 1, at)
            for slab in range(1, slabs - 1):
                after = bricks.load(piece, slab + 1, at)
                side = bricks.lateral(shader, piece, slab, at, here)
                cells_here.append((here, after - before, *side))
                before, here = here, after
                if len(cells_here) == 2 or slab == slabs - 2:
                    for n, seen_here in enumerate(shader.look(cells_here)):
                        state = shader.add(state, start <= slab + 1 - len(cells_here) + n, *seen_here)
                    cells_here = []
            to = pl.ds(at - ROW, ROW)
            for k in range(3):
                seen[piece, k, to, :] = state[1] + state[2][k]
            seen[piece, 3, to, :] = state[0]
            for end, (slab, inner) in enumerate(((0, 1), (slabs - 1, slabs - 2))):
                side = bricks.lateral(shader, piece, slab, at, bricks.load(piece, slab, at))
                for k, value in enumerate((*side, bricks.load(piece, inner, at))):
                    ends[end, k, piece, to, :] = value
        return carry

    lax.fori_loop(0, pieces, column, 0)


def finish_kernel(
    depth_total, light, transfer, base, volume, entry, above, below, front, back, near, far, seen, ends, out, upper, lower, sems
):
    slabs, rows, columns = volume.shape
    pieces = columns // LANE
    at_last = rows - ROW

    def fetches(piece):
        cols = pl.ds(pl.multiple_of(piece * LANE, LANE), LANE)
        return (
            pltpu.make_async_copy(
                volume.at[:, pl.ds(0, 2 * ROW), cols], upper.at[piece + 1, :, pl.ds(ROW, 2 * ROW), :], sems.at[0, piece]
            ),
            pltpu.make_async_copy(
                volume.at[:, pl.ds(rows - 2 * ROW, 2 * ROW), cols], lower.at[piece + 1, :, pl.ds(0, 2 * ROW), :], sems.at[1, piece]
            ),
        )

    def begin(piece, carry):
        for copy in fetches(piece):
            copy.start()
        return carry

    lax.fori_loop(0, pieces, begin, 0)
    shader = Shader(light, transfer, depth_total)
    lanes = lax.broadcasted_iota(jnp.int32, (ROW, LANE), 1)
    tops, bottoms = Bricks(upper, lanes), Bricks(lower, lanes)
    for bricks in (tops, bottoms):
        bricks.clear_sides(ROW, ROW)
    origin = base[0]
    zero = jnp.zeros((ROW, LANE), jnp.float32)

    def closing(piece, carry):
        cols = pl.ds(pl.multiple_of(piece * LANE, LANE), LANE)
        for row in range(ROW, at_last, ROW):
            at, src = pl.ds(row, ROW), pl.ds(row - ROW, ROW)
            start = entry[at, cols] - origin
            square, facing, inner = (ends[0, k, piece, src, :] for k in range(3))
            first = (near[at, cols], inner - front[at, cols], square, facing)
            square, facing, inner = (ends[1, k, piece, src, :] for k in range(3))
            last = (far[at, cols], back[at, cols] - inner, square, facing)
            first, last = shader.look_direct(*first), shader.look_direct(*last)
            alpha, plain, tinted = shader.add((zero, zero, [zero] * 3), start <= 0, *first)
            clear = 1.0 - alpha
            tinted = [tinted[k] + plain + clear * seen[piece, k, src, :] for k in range(3)]
            alpha = alpha + clear * seen[piece, 3, src, :]
            alpha, plain, tinted = shader.add((alpha, zero, tinted), start <= slabs - 1, *last)
            for k in range(3):
                out[piece, k, at, :] = plain + tinted[k]
            out[piece, 3, at, :] = alpha
        return carry

    lax.fori_loop(0, pieces, closing, 0)

    def ready(piece, carry):
        for copy in fetches(piece):
            copy.wait()
        cols = pl.ds(pl.multiple_of(piece * LANE, LANE), LANE)
        for slab in range(slabs):
            upper[piece + 1, slab, ROW - 1 : ROW, :] = above[slab, :, cols]
            lower[piece + 1, slab, 2 * ROW : 2 * ROW + 1, :] = below[slab, :, cols]
        return carry

    lax.fori_loop(0, pieces, ready, 0)

    def rims(piece, carry):
        cols = pl.ds(pl.multiple_of(piece * LANE, LANE), LANE)
        for bricks, row in ((tops, 0), (bottoms, at_last)):
            at = pl.ds(row, ROW)
            start = entry[at, cols] - origin
            state = (zero, zero, [zero] * 3)
            cells_here = []
            before, here = front[at, cols], bricks.load(piece, 0, ROW)
            for slab in range(slabs):
                after = back[at, cols] if slab == slabs - 1 else bricks.load(piece, slab + 1, ROW)
                side = bricks.lateral(shader, piece, slab, ROW, here)
                cells_here.append((here, after - before, *side))
                before, here = here, after
                if len(cells_here) == 2 or slab == slabs - 1:
                    for n, seen_here in enumerate(shader.look(cells_here)):
                        state = shader.add(state, start <= slab + 1 - len(cells_here) + n, *seen_here)
                    cells_here = []
            alpha, plain, tinted = state
            for k in range(3):
                out[piece, k, at, :] = plain + tinted[k]
            out[piece, 3, at, :] = alpha
        return carry

    lax.fori_loop(0, pieces, rims, 0, unroll=2)


def middle(volume, entry, light, transfer, base, depth_total):
    slabs, rows, columns = volume.shape
    pieces, inner = columns // LANE, rows - 2 * ROW
    work = (slabs - 2) * inner * columns
    return pl.pallas_call(
        functools.partial(middle_kernel, depth_total),
        in_specs=[SMEM, SMEM, SMEM, HBM, VMEM],
        out_specs=[VMEM, VMEM],
        out_shape=[
            jax.ShapeDtypeStruct((pieces, CHANNELS, inner, LANE), jnp.float32),
            jax.ShapeDtypeStruct((2, 3, pieces, inner, LANE), jnp.float32),
        ],
        scratch_shapes=[
            pltpu.VMEM((pieces + 2, slabs, rows, LANE), jnp.float32),
            pltpu.SemaphoreType.DMA((pieces,)),
        ],
        compiler_params=pltpu.CompilerParams(vmem_limit_bytes=46 * 2**20),
        cost_estimate=pl.CostEstimate(flops=work * 60, bytes_accessed=work * 4, transcendentals=work * 6),
        name="middle",
    )(light, transfer, base, volume, entry)


def finish(volume, entry, above, below, front, back, near, far, seen, ends, light, transfer, base, depth_total):
    slabs, rows, columns = volume.shape
    pieces = columns // LANE
    work = slabs * 2 * ROW * columns + 2 * rows * columns
    rim = pltpu.VMEM((pieces + 2, slabs, 3 * ROW, LANE), jnp.float32)
    return pl.pallas_call(
        functools.partial(finish_kernel, depth_total),
        in_specs=[SMEM] * 3 + [HBM] + [VMEM] * 9,
        out_specs=VMEM,
        out_shape=jax.ShapeDtypeStruct((pieces, CHANNELS, rows, LANE), jnp.float32),
        scratch_shapes=[rim, rim, pltpu.SemaphoreType.DMA((2, pieces))],
        compiler_params=pltpu.CompilerParams(vmem_limit_bytes=40 * 2**20),
        cost_estimate=pl.CostEstimate(flops=work * 60, bytes_accessed=work * 4, transcendentals=work * 6),
        name="finish",
    )(light, transfer, base, volume, entry, above, below, front, back, near, far, seen, ends)


def merge_kernel(parts, out):
    count, _, rows, _ = parts.shape

    def rows_of(tile, carry):
        at = pl.ds(pl.multiple_of(tile * ROW, ROW), ROW)
        clear = 1.0 - parts[0, 3, at, :]
        total = [parts[0, k, at, :] for k in range(CHANNELS)]
        for d in range(1, count):
            total = [total[k] + clear * parts[d, k, at, :] for k in range(CHANNELS)]
            clear = clear - clear * parts[d, 3, at, :]
        for k in range(CHANNELS):
            out[k, at, :] = total[k]
        return carry

    lax.fori_loop(0, rows // ROW, rows_of, 0, unroll=2)


def merge(parts):
    _, channels, rows, cols = parts.shape
    return pl.pallas_call(
        merge_kernel,
        in_specs=[VMEM],
        out_specs=VMEM,
        out_shape=jax.ShapeDtypeStruct((channels, rows, cols), jnp.float32),
        compiler_params=pltpu.CompilerParams(vmem_limit_bytes=8 * 2**20),
        cost_estimate=pl.CostEstimate(flops=parts.size, bytes_accessed=parts.size * 4, transcendentals=0),
        name="merge",
    )(parts)


def local(volume, entry, light, transfer):
    slabs, _, _ = volume.shape
    groups, tiles = lax.axis_size("depth"), lax.axis_size("tile")
    total = float(slabs * groups)
    up = [(i, i + 1) for i in range(groups - 1)]
    up_t = [(i, i + 1) for i in range(tiles - 1)]
    last_slab, first_slab, last_row, first_row = edges(volume)
    front = lax.ppermute(last_slab, "depth", up)
    back = lax.ppermute(first_slab, "depth", [(b, a) for a, b in up])
    above = lax.ppermute(last_row, "tile", up_t)
    below = lax.ppermute(first_row, "tile", [(b, a) for a, b in up_t])
    base = jnp.full((1,), lax.axis_index("depth") * slabs, jnp.int32)

    seen, ends = middle(volume, entry, light, transfer, base, total)
    parts = finish(
        volume, entry, above, below, front, back, first_slab, last_slab, seen, ends, light, transfer, base, total
    )
    return merge(lax.all_to_all(parts, "depth", 0, 0))


def solution(mesh):
    placed = (P("depth", "tile", None), P("tile", None), P(), P())
    return jax.shard_map(local, mesh=mesh, in_specs=placed, out_specs=P(None, "tile", "depth"), check_vma=False)
```

```python
import functools
import math

import jax
import jax.numpy as jnp
from jax import lax
from jax.experimental import pallas as pl
from jax.experimental.pallas import tpu as pltpu
from jax.sharding import PartitionSpec as P

ROW = 8
LANE = 128
LOG2E = 1.4426950408889634
CHANNELS = 4
GROUP = 2
VMEM = pl.BlockSpec(memory_space=pltpu.VMEM)
SMEM = pl.BlockSpec(memory_space=pltpu.SMEM)
HBM = pl.BlockSpec(memory_space=pl.ANY)


def edges_kernel(volume, last_slab, first_slab, last_row, first_row, sems):
    slabs, rows, _ = volume.shape
    copies = [
        pltpu.make_async_copy(volume.at[slabs - 1], last_slab, sems.at[0]),
        pltpu.make_async_copy(volume.at[0], first_slab, sems.at[1]),
        pltpu.make_async_copy(volume.at[:, pl.ds(rows - 1, 1), :], last_row, sems.at[2]),
        pltpu.make_async_copy(volume.at[:, pl.ds(0, 1), :], first_row, sems.at[3]),
    ]
    for copy in copies:
        copy.start()
    for copy in copies:
        copy.wait()


def edges(volume):
    slabs, rows, columns = volume.shape
    slab = jax.ShapeDtypeStruct((rows, columns), jnp.float32)
    row = jax.ShapeDtypeStruct((slabs, 1, columns), jnp.float32)
    return pl.pallas_call(
        edges_kernel,
        in_specs=[HBM],
        out_specs=[VMEM] * 4,
        out_shape=[slab, slab, row, row],
        scratch_shapes=[pltpu.SemaphoreType.DMA((4,))],
        compiler_params=pltpu.CompilerParams(vmem_limit_bytes=50 * 2**20),
        cost_estimate=pl.CostEstimate(flops=0, bytes_accessed=4 * 2**20, transcendentals=0),
        name="edges",
    )(volume)


def constants(light, transfer):
    def splat(value):
        return jnp.full((ROW, LANE), value, jnp.float32)

    toward = [splat(light[i]) for i in range(3)]
    scale = 0.35 * lax.rsqrt(toward[0] * toward[0] + toward[1] * toward[1] + toward[2] * toward[2])
    toward = [value * scale for value in toward]
    rows = [[transfer[k, i] * (0.25 if i == 1 else 0.5) for i in range(3)] for k in range(3)]
    rows.append([transfer[3, i] * (-0.5 * LOG2E if i == 1 else -LOG2E) for i in range(3)])
    return toward, rows


def mixing(rows, width):
    size = (CHANNELS * ROW, 10 * ROW)
    line = lax.broadcasted_iota(jnp.int32, size, 0)
    column = lax.broadcasted_iota(jnp.int32, size, 1)
    block, diagonal = column >> 3, (column & 7) == (line & 7)
    shift = jnp.full(size, width, jnp.float32)

    def chosen(i):
        value = jnp.full(size, rows[0][i], jnp.float32)
        for k in range(1, CHANNELS):
            value = jnp.where(line >= k * ROW, rows[k][i], value)
        return value

    def top(value):
        return value.astype(jnp.bfloat16).astype(jnp.float32)

    scale = jnp.where((block & 1) == 0, chosen(0), chosen(1))
    scale = jnp.where(block < 4, top(scale), scale - top(scale))
    offset = chosen(2) + jnp.where(line >= 3 * ROW, shift, 0.0)
    high = top(offset)
    low = top(offset - high)
    offset = jnp.where(column == 8 * ROW, high, jnp.where(column == 8 * ROW + 1, low, offset - high - low))
    mix = jnp.where((block < 8) & diagonal, scale, jnp.where((column >= 8 * ROW) & (column < 8 * ROW + 3), offset, 0.0))
    return mix.astype(jnp.bfloat16)


class Shader:
    def __init__(self, light, transfer, depth_total):
        self.toward, rows = constants(light, transfer)
        self.bound = depth_total / 4.0
        width = math.log2(depth_total / 4.0)
        self.rows = [
            [jnp.full((ROW, LANE), row[i] + (width if (k, i) == (3, 2) else 0.0), jnp.float32) for i in range(3)]
            for k, row in enumerate(rows)
        ]
        self.mix = mixing(rows, width)
        self.ones = jnp.ones((2 * ROW, LANE), jnp.bfloat16)

    def lateral(self, gx, gy):
        return gx * gx + gy * gy + 4.0, self.toward[1] * gx + self.toward[2] * gy

    def look(self, cells):
        pairs, shades = [], []
        for here, gz, square, facing in cells:
            square = square + gz * gz
            inverse = lax.rsqrt(square)
            pairs.append(jnp.concatenate([here, square * inverse], axis=0))
            shades.append(0.15 + jnp.abs(self.toward[0] * gz + facing) * inverse)
        pair = jnp.concatenate(pairs, axis=1)
        high = pair.astype(jnp.bfloat16)
        low = (pair - high.astype(jnp.float32)).astype(jnp.bfloat16)
        ones = jnp.concatenate([self.ones] * len(cells), axis=1)
        terms = jnp.concatenate([high, low, high, low, ones], axis=0)
        args = jnp.dot(self.mix, terms, preferred_element_type=jnp.float32)
        args = [
            [args[k * ROW : (k + 1) * ROW, n * LANE : (n + 1) * LANE] for k in range(CHANNELS)] for n in range(len(cells))
        ]
        return list(zip(shades, args))

    def look_direct(self, here, gz, square, facing):
        square = square + gz * gz
        inverse = lax.rsqrt(square)
        norm = square * inverse
        shade = 0.15 + jnp.abs(self.toward[0] * gz + facing) * inverse
        return shade, [self.rows[k][0] * here + self.rows[k][1] * norm + self.rows[k][2] for k in range(CHANNELS)]

    def add(self, state, visible, shade, args):
        alpha, plain, tinted = state
        root = lax.rsqrt(jnp.exp2(args[3]) + self.bound)
        opacity = jnp.where(visible, root * root, 0.0)
        weight = opacity - alpha * opacity
        lit = weight * shade
        tinted = [tinted[k] + lit * jnp.tanh(args[k]) for k in range(3)]
        return alpha + weight, plain + lit, tinted


class Bricks:
    def __init__(self, cells, lanes):
        self.cells = cells
        self.left_edge, self.right_edge = lanes == 0, lanes == LANE - 1

    def load(self, piece, slab, at, shift=0, aside=0):
        return self.cells[piece + 1 + aside, slab, pl.ds(at + shift, ROW), :]

    def lateral(self, shader, piece, slab, at, here):
        lf = pltpu.roll(jnp.where(self.right_edge, self.load(piece, slab, at, 0, -1), here), 1, 1)
        rt = pltpu.roll(jnp.where(self.left_edge, self.load(piece, slab, at, 0, 1), here), LANE - 1, 1)
        return shader.lateral(self.load(piece, slab, at, 1) - self.load(piece, slab, at, -1), rt - lf)

    def clear_sides(self, at, rows):
        pieces, slabs = self.cells.shape[0] - 2, self.cells.shape[1]
        blank = jnp.zeros((rows, LANE), jnp.float32)
        for slab in range(slabs):
            self.cells[0, slab, at : at + rows] = blank
            self.cells[pieces + 1, slab, at : at + rows] = blank


def middle_kernel(depth_total, light, transfer, base, volume, entry, seen, ends, cells, sems):
    slabs, rows, columns = volume.shape
    pieces = columns // LANE

    def fetch(piece):
        return pltpu.make_async_copy(
            volume.at[:, :, pl.ds(pl.multiple_of(piece * LANE, LANE), LANE)],
            cells.at[piece + 1],
            sems.at[piece],
        )

    def begin(piece, carry):
        fetch(piece).start()
        return carry

    lax.fori_loop(0, pieces, begin, 0)
    bricks = Bricks(cells, lax.broadcasted_iota(jnp.int32, (ROW, LANE), 1))
    bricks.clear_sides(ROW, rows - 2 * ROW)
    shader = Shader(light, transfer, depth_total)
    origin = base[0]
    zero = jnp.zeros((ROW, LANE), jnp.float32)
    fetch(0).wait()

    def columns_of(group, carry):
        for member in range(1, GROUP):
            fetch(group * GROUP + member).wait()

        @pl.when(group < pieces // GROUP - 1)
        def _():
            fetch(group * GROUP + GROUP).wait()

        for member in range(GROUP):
            piece = group * GROUP + member
            cols = pl.ds(pl.multiple_of(piece * LANE, LANE), LANE)
            for at in range(ROW, rows - ROW, ROW):
                start = entry[at : at + ROW, cols] - origin
                state = (zero, zero, [zero] * 3)
                cells_here = []
                before, here = bricks.load(piece, 0, at), bricks.load(piece, 1, at)
                for slab in range(1, slabs - 1):
                    after = bricks.load(piece, slab + 1, at)
                    side = bricks.lateral(shader, piece, slab, at, here)
                    cells_here.append((here, after - before, *side))
                    before, here = here, after
                    if len(cells_here) == 2 or slab == slabs - 2:
                        for n, seen_here in enumerate(shader.look(cells_here)):
                            state = shader.add(state, start <= slab + 1 - len(cells_here) + n, *seen_here)
                        cells_here = []
                to = pl.ds(at - ROW, ROW)
                for k in range(3):
                    seen[piece, k, to, :] = state[1] + state[2][k]
                seen[piece, 3, to, :] = state[0]
                for end, (slab, inner) in enumerate(((0, 1), (slabs - 1, slabs - 2))):
                    side = bricks.lateral(shader, piece, slab, at, bricks.load(piece, slab, at))
                    for k, value in enumerate((*side, bricks.load(piece, inner, at))):
                        ends[end, k, piece, to, :] = value
        return carry

    lax.fori_loop(0, pieces // GROUP, columns_of, 0)


def finish_kernel(
    depth_total, light, transfer, base, volume, entry, above, below, front, back, near, far, seen, ends, out, upper, lower, sems
):
    slabs, rows, columns = volume.shape
    pieces = columns // LANE
    at_last = rows - ROW

    def fetches(piece):
        cols = pl.ds(pl.multiple_of(piece * LANE, LANE), LANE)
        return (
            pltpu.make_async_copy(
                volume.at[:, pl.ds(0, 2 * ROW), cols], upper.at[piece + 1, :, pl.ds(ROW, 2 * ROW), :], sems.at[0, piece]
            ),
            pltpu.make_async_copy(
                volume.at[:, pl.ds(rows - 2 * ROW, 2 * ROW), cols], lower.at[piece + 1, :, pl.ds(0, 2 * ROW), :], sems.at[1, piece]
            ),
        )

    def begin(piece, carry):
        for copy in fetches(piece):
            copy.start()
        return carry

    lax.fori_loop(0, pieces, begin, 0)
    shader = Shader(light, transfer, depth_total)
    lanes = lax.broadcasted_iota(jnp.int32, (ROW, LANE), 1)
    tops, bottoms = Bricks(upper, lanes), Bricks(lower, lanes)
    for bricks in (tops, bottoms):
        bricks.clear_sides(ROW, ROW)
    origin = base[0]
    zero = jnp.zeros((ROW, LANE), jnp.float32)

    def closing(piece, carry):
        cols = pl.ds(pl.multiple_of(piece * LANE, LANE), LANE)
        for row in range(ROW, at_last, ROW):
            at, src = pl.ds(row, ROW), pl.ds(row - ROW, ROW)
            start = entry[at, cols] - origin
            square, facing, inner = (ends[0, k, piece, src, :] for k in range(3))
            first = (near[at, cols], inner - front[at, cols], square, facing)
            square, facing, inner = (ends[1, k, piece, src, :] for k in range(3))
            last = (far[at, cols], back[at, cols] - inner, square, facing)
            first, last = shader.look_direct(*first), shader.look_direct(*last)
            alpha, plain, tinted = shader.add((zero, zero, [zero] * 3), start <= 0, *first)
            clear = 1.0 - alpha
            tinted = [tinted[k] + plain + clear * seen[piece, k, src, :] for k in range(3)]
            alpha = alpha + clear * seen[piece, 3, src, :]
            alpha, plain, tinted = shader.add((alpha, zero, tinted), start <= slabs - 1, *last)
            for k in range(3):
                out[piece, k, at, :] = plain + tinted[k]
            out[piece, 3, at, :] = alpha
        return carry

    lax.fori_loop(0, pieces, closing, 0)

    def ready(piece, carry):
        for copy in fetches(piece):
            copy.wait()
        cols = pl.ds(pl.multiple_of(piece * LANE, LANE), LANE)
        for slab in range(slabs):
            upper[piece + 1, slab, ROW - 1 : ROW, :] = above[slab, :, cols]
            lower[piece + 1, slab, 2 * ROW : 2 * ROW + 1, :] = below[slab, :, cols]
        return carry

    lax.fori_loop(0, pieces, ready, 0)

    def rims(piece, carry):
        cols = pl.ds(pl.multiple_of(piece * LANE, LANE), LANE)
        for bricks, row in ((tops, 0), (bottoms, at_last)):
            at = pl.ds(row, ROW)
            start = entry[at, cols] - origin
            state = (zero, zero, [zero] * 3)
            cells_here = []
            before, here = front[at, cols], bricks.load(piece, 0, ROW)
            for slab in range(slabs):
                after = back[at, cols] if slab == slabs - 1 else bricks.load(piece, slab + 1, ROW)
                side = bricks.lateral(shader, piece, slab, ROW, here)
                cells_here.append((here, after - before, *side))
                before, here = here, after
                if len(cells_here) == 2 or slab == slabs - 1:
                    for n, seen_here in enumerate(shader.look(cells_here)):
                        state = shader.add(state, start <= slab + 1 - len(cells_here) + n, *seen_here)
                    cells_here = []
            alpha, plain, tinted = state
            for k in range(3):
                out[piece, k, at, :] = plain + tinted[k]
            out[piece, 3, at, :] = alpha
        return carry

    lax.fori_loop(0, pieces, rims, 0, unroll=8)


def middle(volume, entry, light, transfer, base, depth_total):
    slabs, rows, columns = volume.shape
    pieces, inner = columns // LANE, rows - 2 * ROW
    work = (slabs - 2) * inner * columns
    return pl.pallas_call(
        functools.partial(middle_kernel, depth_total),
        in_specs=[SMEM, SMEM, SMEM, HBM, VMEM],
        out_specs=[VMEM, VMEM],
        out_shape=[
            jax.ShapeDtypeStruct((pieces, CHANNELS, inner, LANE), jnp.float32),
            jax.ShapeDtypeStruct((2, 3, pieces, inner, LANE), jnp.float32),
        ],
        scratch_shapes=[
            pltpu.VMEM((pieces + 2, slabs, rows, LANE), jnp.float32),
            pltpu.SemaphoreType.DMA((pieces,)),
        ],
        compiler_params=pltpu.CompilerParams(vmem_limit_bytes=46 * 2**20),
        cost_estimate=pl.CostEstimate(flops=work * 60, bytes_accessed=work * 4, transcendentals=work * 6),
        name="middle",
    )(light, transfer, base, volume, entry)


def finish(volume, entry, above, below, front, back, near, far, seen, ends, light, transfer, base, depth_total):
    slabs, rows, columns = volume.shape
    pieces = columns // LANE
    work = slabs * 2 * ROW * columns + 2 * rows * columns
    rim = pltpu.VMEM((pieces + 2, slabs, 3 * ROW, LANE), jnp.float32)
    return pl.pallas_call(
        functools.partial(finish_kernel, depth_total),
        in_specs=[SMEM] * 3 + [HBM] + [VMEM] * 9,
        out_specs=VMEM,
        out_shape=jax.ShapeDtypeStruct((pieces, CHANNELS, rows, LANE), jnp.float32),
        scratch_shapes=[rim, rim, pltpu.SemaphoreType.DMA((2, pieces))],
        compiler_params=pltpu.CompilerParams(vmem_limit_bytes=40 * 2**20),
        cost_estimate=pl.CostEstimate(flops=work * 60, bytes_accessed=work * 4, transcendentals=work * 6),
        name="finish",
    )(light, transfer, base, volume, entry, above, below, front, back, near, far, seen, ends)


def merge_kernel(parts, out):
    count, _, rows, _ = parts.shape

    def rows_of(tile, carry):
        at = pl.ds(pl.multiple_of(tile * ROW, ROW), ROW)
        clear = 1.0 - parts[0, 3, at, :]
        total = [parts[0, k, at, :] for k in range(CHANNELS)]
        for d in range(1, count):
            total = [total[k] + clear * parts[d, k, at, :] for k in range(CHANNELS)]
            clear = clear - clear * parts[d, 3, at, :]
        for k in range(CHANNELS):
            out[k, at, :] = total[k]
        return carry

    lax.fori_loop(0, rows // ROW, rows_of, 0, unroll=2)


def merge(parts):
    _, channels, rows, cols = parts.shape
    return pl.pallas_call(
        merge_kernel,
        in_specs=[VMEM],
        out_specs=VMEM,
        out_shape=jax.ShapeDtypeStruct((channels, rows, cols), jnp.float32),
        compiler_params=pltpu.CompilerParams(vmem_limit_bytes=8 * 2**20),
        cost_estimate=pl.CostEstimate(flops=parts.size, bytes_accessed=parts.size * 4, transcendentals=0),
        name="merge",
    )(parts)


def local(volume, entry, light, transfer):
    slabs, _, _ = volume.shape
    groups, tiles = lax.axis_size("depth"), lax.axis_size("tile")
    total = float(slabs * groups)
    up = [(i, i + 1) for i in range(groups - 1)]
    up_t = [(i, i + 1) for i in range(tiles - 1)]
    last_slab, first_slab, last_row, first_row = edges(volume)
    front = lax.ppermute(last_slab, "depth", up)
    back = lax.ppermute(first_slab, "depth", [(b, a) for a, b in up])
    above = lax.ppermute(last_row, "tile", up_t)
    below = lax.ppermute(first_row, "tile", [(b, a) for a, b in up_t])
    base = jnp.full((1,), lax.axis_index("depth") * slabs, jnp.int32)

    seen, ends = middle(volume, entry, light, transfer, base, total)
    parts = finish(
        volume, entry, above, below, front, back, first_slab, last_slab, seen, ends, light, transfer, base, total
    )
    return merge(lax.all_to_all(parts, "depth", 0, 0))


def solution(mesh):
    placed = (P("depth", "tile", None), P("tile", None), P(), P())
    return jax.shard_map(local, mesh=mesh, in_specs=placed, out_specs=P(None, "tile", "depth"), check_vma=False)
```

```python
import functools
import math

import jax
import jax.numpy as jnp
from jax import lax
from jax.experimental import pallas as pl
from jax.experimental.pallas import tpu as pltpu
from jax.sharding import PartitionSpec as P

ROW = 8
LANE = 128
LOG2E = 1.4426950408889634
CHANNELS = 4
GROUP = 2
VMEM = pl.BlockSpec(memory_space=pltpu.VMEM)
SMEM = pl.BlockSpec(memory_space=pltpu.SMEM)
HBM = pl.BlockSpec(memory_space=pl.ANY)


def edges_kernel(volume, last_slab, first_slab, last_row, first_row, sems):
    slabs, rows, _ = volume.shape
    copies = [
        pltpu.make_async_copy(volume.at[slabs - 1], last_slab, sems.at[0]),
        pltpu.make_async_copy(volume.at[0], first_slab, sems.at[1]),
        pltpu.make_async_copy(volume.at[:, pl.ds(rows - 1, 1), :], last_row, sems.at[2]),
        pltpu.make_async_copy(volume.at[:, pl.ds(0, 1), :], first_row, sems.at[3]),
    ]
    for copy in copies:
        copy.start()
    for copy in copies:
        copy.wait()


def edges(volume):
    slabs, rows, columns = volume.shape
    slab = jax.ShapeDtypeStruct((rows, columns), jnp.float32)
    row = jax.ShapeDtypeStruct((slabs, 1, columns), jnp.float32)
    return pl.pallas_call(
        edges_kernel,
        in_specs=[HBM],
        out_specs=[VMEM] * 4,
        out_shape=[slab, slab, row, row],
        scratch_shapes=[pltpu.SemaphoreType.DMA((4,))],
        compiler_params=pltpu.CompilerParams(vmem_limit_bytes=50 * 2**20),
        cost_estimate=pl.CostEstimate(flops=0, bytes_accessed=4 * 2**20, transcendentals=0),
        name="edges",
    )(volume)


def constants(light, transfer):
    def splat(value):
        return jnp.full((ROW, LANE), value, jnp.float32)

    toward = [splat(light[i]) for i in range(3)]
    scale = 0.35 * lax.rsqrt(toward[0] * toward[0] + toward[1] * toward[1] + toward[2] * toward[2])
    toward = [value * scale for value in toward]
    rows = [[transfer[k, i] * (0.25 if i == 1 else 0.5) for i in range(3)] for k in range(3)]
    rows.append([transfer[3, i] * (-0.5 * LOG2E if i == 1 else -LOG2E) for i in range(3)])
    return toward, rows


def mixing(rows, width):
    size = (CHANNELS * ROW, 10 * ROW)
    line = lax.broadcasted_iota(jnp.int32, size, 0)
    column = lax.broadcasted_iota(jnp.int32, size, 1)
    block, diagonal = column >> 3, (column & 7) == (line & 7)
    shift = jnp.full(size, width, jnp.float32)

    def chosen(i):
        value = jnp.full(size, rows[0][i], jnp.float32)
        for k in range(1, CHANNELS):
            value = jnp.where(line >= k * ROW, rows[k][i], value)
        return value

    def top(value):
        return value.astype(jnp.bfloat16).astype(jnp.float32)

    scale = jnp.where((block & 1) == 0, chosen(0), chosen(1))
    scale = jnp.where(block < 4, top(scale), scale - top(scale))
    offset = chosen(2) + jnp.where(line >= 3 * ROW, shift, 0.0)
    high = top(offset)
    low = top(offset - high)
    offset = jnp.where(column == 8 * ROW, high, jnp.where(column == 8 * ROW + 1, low, offset - high - low))
    mix = jnp.where((block < 8) & diagonal, scale, jnp.where((column >= 8 * ROW) & (column < 8 * ROW + 3), offset, 0.0))
    return mix.astype(jnp.bfloat16)


class Shader:
    def __init__(self, light, transfer, depth_total):
        self.toward, rows = constants(light, transfer)
        self.bound = depth_total / 4.0
        width = math.log2(depth_total / 4.0)
        self.rows = [
            [jnp.full((ROW, LANE), row[i] + (width if (k, i) == (3, 2) else 0.0), jnp.float32) for i in range(3)]
            for k, row in enumerate(rows)
        ]
        self.mix = mixing(rows, width)
        self.ones = jnp.ones((2 * ROW, LANE), jnp.bfloat16)

    def lateral(self, gx, gy):
        return gx * gx + gy * gy + 4.0, self.toward[1] * gx + self.toward[2] * gy

    def look(self, cells):
        pairs, shades = [], []
        for here, gz, square, facing in cells:
            square = square + gz * gz
            inverse = lax.rsqrt(square)
            pairs.append(jnp.concatenate([here, square * inverse], axis=0))
            shades.append(0.15 + jnp.abs(self.toward[0] * gz + facing) * inverse)
        pair = jnp.concatenate(pairs, axis=1)
        high = pair.astype(jnp.bfloat16)
        low = (pair - high.astype(jnp.float32)).astype(jnp.bfloat16)
        ones = jnp.concatenate([self.ones] * len(cells), axis=1)
        terms = jnp.concatenate([high, low, high, low, ones], axis=0)
        args = jnp.dot(self.mix, terms, preferred_element_type=jnp.float32)
        args = [
            [args[k * ROW : (k + 1) * ROW, n * LANE : (n + 1) * LANE] for k in range(CHANNELS)] for n in range(len(cells))
        ]
        return list(zip(shades, args))

    def look_direct(self, here, gz, square, facing):
        square = square + gz * gz
        inverse = lax.rsqrt(square)
        norm = square * inverse
        shade = 0.15 + jnp.abs(self.toward[0] * gz + facing) * inverse
        return shade, [self.rows[k][0] * here + self.rows[k][1] * norm + self.rows[k][2] for k in range(CHANNELS)]

    def add(self, state, visible, shade, args):
        alpha, plain, tinted = state
        root = lax.rsqrt(jnp.exp2(args[3]) + self.bound)
        opacity = jnp.where(visible, root * root, 0.0)
        weight = opacity - alpha * opacity
        lit = weight * shade
        tinted = [tinted[k] + lit * jnp.tanh(args[k]) for k in range(3)]
        return alpha + weight, plain + lit, tinted


class Bricks:
    def __init__(self, cells, lanes):
        self.cells = cells
        self.left_edge, self.right_edge = lanes == 0, lanes == LANE - 1

    def load(self, piece, slab, at, shift=0, aside=0):
        return self.cells[piece + 1 + aside, slab, pl.ds(at + shift, ROW), :]

    def lateral(self, shader, piece, slab, at, here):
        lf = pltpu.roll(jnp.where(self.right_edge, self.load(piece, slab, at, 0, -1), here), 1, 1)
        rt = pltpu.roll(jnp.where(self.left_edge, self.load(piece, slab, at, 0, 1), here), LANE - 1, 1)
        return shader.lateral(self.load(piece, slab, at, 1) - self.load(piece, slab, at, -1), rt - lf)

    def clear_sides(self, at, rows):
        pieces, slabs = self.cells.shape[0] - 2, self.cells.shape[1]
        blank = jnp.zeros((rows, LANE), jnp.float32)
        for slab in range(slabs):
            self.cells[0, slab, at : at + rows] = blank
            self.cells[pieces + 1, slab, at : at + rows] = blank


def middle_kernel(depth_total, light, transfer, base, volume, entry, seen, ends, cells, sems):
    slabs, rows, columns = volume.shape
    pieces = columns // LANE

    def fetch(piece):
        return pltpu.make_async_copy(
            volume.at[:, :, pl.ds(pl.multiple_of(piece * LANE, LANE), LANE)],
            cells.at[piece + 1],
            sems.at[piece],
        )

    def begin(piece, carry):
        fetch(piece).start()
        return carry

    lax.fori_loop(0, pieces, begin, 0)
    bricks = Bricks(cells, lax.broadcasted_iota(jnp.int32, (ROW, LANE), 1))
    bricks.clear_sides(ROW, rows - 2 * ROW)
    shader = Shader(light, transfer, depth_total)
    origin = base[0]
    zero = jnp.zeros((ROW, LANE), jnp.float32)
    fetch(0).wait()

    def columns_of(group, carry):
        for member in range(1, GROUP):
            fetch(group * GROUP + member).wait()

        @pl.when(group < pieces // GROUP - 1)
        def _():
            fetch(group * GROUP + GROUP).wait()

        for member in range(GROUP):
            piece = group * GROUP + member
            cols = pl.ds(pl.multiple_of(piece * LANE, LANE), LANE)
            for at in range(ROW, rows - ROW, ROW):
                start = entry[at : at + ROW, cols] - origin
                state = (zero, zero, [zero] * 3)
                cells_here = []
                before, here = bricks.load(piece, 0, at), bricks.load(piece, 1, at)
                for slab in range(1, slabs - 1):
                    after = bricks.load(piece, slab + 1, at)
                    side = bricks.lateral(shader, piece, slab, at, here)
                    cells_here.append((here, after - before, *side))
                    before, here = here, after
                    if len(cells_here) == 2 or slab == slabs - 2:
                        for n, seen_here in enumerate(shader.look(cells_here)):
                            state = shader.add(state, start <= slab + 1 - len(cells_here) + n, *seen_here)
                        cells_here = []
                to = pl.ds(at - ROW, ROW)
                for k in range(3):
                    seen[piece, k, to, :] = state[1] + state[2][k]
                seen[piece, 3, to, :] = state[0]
                for end, (slab, inner) in enumerate(((0, 1), (slabs - 1, slabs - 2))):
                    side = bricks.lateral(shader, piece, slab, at, bricks.load(piece, slab, at))
                    for k, value in enumerate((*side, bricks.load(piece, inner, at))):
                        ends[end, k, piece, to, :] = value
        return carry

    lax.fori_loop(0, pieces // GROUP, columns_of, 0)


def finish_kernel(
    depth_total, light, transfer, base, volume, entry, above, below, front, back, near, far, seen, ends, out, upper, lower, sems
):
    slabs, rows, columns = volume.shape
    pieces = columns // LANE
    at_last = rows - ROW

    def fetches(piece):
        cols = pl.ds(pl.multiple_of(piece * LANE, LANE), LANE)
        return (
            pltpu.make_async_copy(
                volume.at[:, pl.ds(0, 2 * ROW), cols], upper.at[piece + 1, :, pl.ds(ROW, 2 * ROW), :], sems.at[0, piece]
            ),
            pltpu.make_async_copy(
                volume.at[:, pl.ds(rows - 2 * ROW, 2 * ROW), cols], lower.at[piece + 1, :, pl.ds(0, 2 * ROW), :], sems.at[1, piece]
            ),
        )

    def begin(piece, carry):
        for copy in fetches(piece):
            copy.start()
        return carry

    lax.fori_loop(0, pieces, begin, 0)
    shader = Shader(light, transfer, depth_total)
    lanes = lax.broadcasted_iota(jnp.int32, (ROW, LANE), 1)
    tops, bottoms = Bricks(upper, lanes), Bricks(lower, lanes)
    for bricks in (tops, bottoms):
        bricks.clear_sides(ROW, ROW)
    origin = base[0]
    zero = jnp.zeros((ROW, LANE), jnp.float32)

    def closing(piece, carry):
        cols = pl.ds(pl.multiple_of(piece * LANE, LANE), LANE)
        for row in range(ROW, at_last, ROW):
            at, src = pl.ds(row, ROW), pl.ds(row - ROW, ROW)
            start = entry[at, cols] - origin
            square, facing, inner = (ends[0, k, piece, src, :] for k in range(3))
            first = (near[at, cols], inner - front[at, cols], square, facing)
            square, facing, inner = (ends[1, k, piece, src, :] for k in range(3))
            last = (far[at, cols], back[at, cols] - inner, square, facing)
            first, last = shader.look_direct(*first), shader.look_direct(*last)
            alpha, plain, tinted = shader.add((zero, zero, [zero] * 3), start <= 0, *first)
            clear = 1.0 - alpha
            tinted = [tinted[k] + plain + clear * seen[piece, k, src, :] for k in range(3)]
            alpha = alpha + clear * seen[piece, 3, src, :]
            alpha, plain, tinted = shader.add((alpha, zero, tinted), start <= slabs - 1, *last)
            for k in range(3):
                out[piece, k, at, :] = plain + tinted[k]
            out[piece, 3, at, :] = alpha
        return carry

    lax.fori_loop(0, pieces, closing, 0, unroll=4)

    def ready(piece, carry):
        for copy in fetches(piece):
            copy.wait()
        cols = pl.ds(pl.multiple_of(piece * LANE, LANE), LANE)
        for slab in range(slabs):
            upper[piece + 1, slab, ROW - 1 : ROW, :] = above[slab, :, cols]
            lower[piece + 1, slab, 2 * ROW : 2 * ROW + 1, :] = below[slab, :, cols]
        return carry

    lax.fori_loop(0, pieces, ready, 0, unroll=4)

    def rims(piece, carry):
        cols = pl.ds(pl.multiple_of(piece * LANE, LANE), LANE)
        for bricks, row in ((tops, 0), (bottoms, at_last)):
            at = pl.ds(row, ROW)
            start = entry[at, cols] - origin
            state = (zero, zero, [zero] * 3)
            cells_here = []
            before, here = front[at, cols], bricks.load(piece, 0, ROW)
            for slab in range(slabs):
                after = back[at, cols] if slab == slabs - 1 else bricks.load(piece, slab + 1, ROW)
                side = bricks.lateral(shader, piece, slab, ROW, here)
                cells_here.append((here, after - before, *side))
                before, here = here, after
                if len(cells_here) == 2 or slab == slabs - 1:
                    for n, seen_here in enumerate(shader.look(cells_here)):
                        state = shader.add(state, start <= slab + 1 - len(cells_here) + n, *seen_here)
                    cells_here = []
            alpha, plain, tinted = state
            for k in range(3):
                out[piece, k, at, :] = plain + tinted[k]
            out[piece, 3, at, :] = alpha
        return carry

    lax.fori_loop(0, pieces, rims, 0, unroll=16)


def middle(volume, entry, light, transfer, base, depth_total):
    slabs, rows, columns = volume.shape
    pieces, inner = columns // LANE, rows - 2 * ROW
    work = (slabs - 2) * inner * columns
    return pl.pallas_call(
        functools.partial(middle_kernel, depth_total),
        in_specs=[SMEM, SMEM, SMEM, HBM, VMEM],
        out_specs=[VMEM, VMEM],
        out_shape=[
            jax.ShapeDtypeStruct((pieces, CHANNELS, inner, LANE), jnp.float32),
            jax.ShapeDtypeStruct((2, 3, pieces, inner, LANE), jnp.float32),
        ],
        scratch_shapes=[
            pltpu.VMEM((pieces + 2, slabs, rows, LANE), jnp.float32),
            pltpu.SemaphoreType.DMA((pieces,)),
        ],
        compiler_params=pltpu.CompilerParams(vmem_limit_bytes=46 * 2**20),
        cost_estimate=pl.CostEstimate(flops=work * 60, bytes_accessed=work * 4, transcendentals=work * 6),
        name="middle",
    )(light, transfer, base, volume, entry)


def finish(volume, entry, above, below, front, back, near, far, seen, ends, light, transfer, base, depth_total):
    slabs, rows, columns = volume.shape
    pieces = columns // LANE
    work = slabs * 2 * ROW * columns + 2 * rows * columns
    rim = pltpu.VMEM((pieces + 2, slabs, 3 * ROW, LANE), jnp.float32)
    return pl.pallas_call(
        functools.partial(finish_kernel, depth_total),
        in_specs=[SMEM] * 3 + [HBM] + [VMEM] * 9,
        out_specs=VMEM,
        out_shape=jax.ShapeDtypeStruct((pieces, CHANNELS, rows, LANE), jnp.float32),
        scratch_shapes=[rim, rim, pltpu.SemaphoreType.DMA((2, pieces))],
        compiler_params=pltpu.CompilerParams(vmem_limit_bytes=40 * 2**20),
        cost_estimate=pl.CostEstimate(flops=work * 60, bytes_accessed=work * 4, transcendentals=work * 6),
        name="finish",
    )(light, transfer, base, volume, entry, above, below, front, back, near, far, seen, ends)


def merge_kernel(parts, out):
    count, _, rows, _ = parts.shape

    def rows_of(tile, carry):
        at = pl.ds(pl.multiple_of(tile * ROW, ROW), ROW)
        clear = 1.0 - parts[0, 3, at, :]
        total = [parts[0, k, at, :] for k in range(CHANNELS)]
        for d in range(1, count):
            total = [total[k] + clear * parts[d, k, at, :] for k in range(CHANNELS)]
            clear = clear - clear * parts[d, 3, at, :]
        for k in range(CHANNELS):
            out[k, at, :] = total[k]
        return carry

    lax.fori_loop(0, rows // ROW, rows_of, 0, unroll=8)


def merge(parts):
    _, channels, rows, cols = parts.shape
    return pl.pallas_call(
        merge_kernel,
        in_specs=[VMEM],
        out_specs=VMEM,
        out_shape=jax.ShapeDtypeStruct((channels, rows, cols), jnp.float32),
        compiler_params=pltpu.CompilerParams(vmem_limit_bytes=8 * 2**20),
        cost_estimate=pl.CostEstimate(flops=parts.size, bytes_accessed=parts.size * 4, transcendentals=0),
        name="merge",
    )(parts)


def local(volume, entry, light, transfer):
    slabs, _, _ = volume.shape
    groups, tiles = lax.axis_size("depth"), lax.axis_size("tile")
    total = float(slabs * groups)
    up = [(i, i + 1) for i in range(groups - 1)]
    up_t = [(i, i + 1) for i in range(tiles - 1)]
    last_slab, first_slab, last_row, first_row = edges(volume)
    front = lax.ppermute(last_slab, "depth", up)
    back = lax.ppermute(first_slab, "depth", [(b, a) for a, b in up])
    above = lax.ppermute(last_row, "tile", up_t)
    below = lax.ppermute(first_row, "tile", [(b, a) for a, b in up_t])
    base = jnp.full((1,), lax.axis_index("depth") * slabs, jnp.int32)

    seen, ends = middle(volume, entry, light, transfer, base, total)
    parts = finish(
        volume, entry, above, below, front, back, first_slab, last_slab, seen, ends, light, transfer, base, total
    )
    return merge(lax.all_to_all(parts, "depth", 0, 0))


def solution(mesh):
    placed = (P("depth", "tile", None), P("tile", None), P(), P())
    return jax.shard_map(local, mesh=mesh, in_specs=placed, out_specs=P(None, "tile", "depth"), check_vma=False)
```
